1024 devices in a mesh: wide: 16 (over x_hi, y), narrow: 64 (over z, x_lo, core).
Axes of the slice: x: 4 (x_hi: 2, x_lo: 2; x = x_hi * 2 + x_lo), y: 8, z: 16, core: 2. Of those that a mesh axis runs over, the one named last changes fastest.
Arguments:
- pair_integrals: bfloat16 [65536, 1024], P(('wide', 'narrow')), may hold values from -0.01171875 to 0.01171875
- screening: bfloat16 [1024, 1024], replicated, may hold values from -0.1875 to 0.1875
- virtual_integrals: bfloat16 [1024, 1024, 1024], P(('wide', 'narrow')), may hold values from -0.75 to 0.75
- trials: bfloat16 [1, 256, 1024], P(None, None, 'narrow'), may hold values from -6 to 6
Outputs:
- response: float32 [1024, 1, 256], P('narrow', None, 'wide')
The draws below stay inside these ranges and needn't reach their ends.
All inputs are finite; a program needn't handle non-finite values.
Results may differ from the reference program's by a relative error of at most 0.0041.
Values may be sent and summed in bfloat16 or wider, within the bound.
No kernel may reach another device: no remote copies, remote signals or barrier semaphores. Data moves between devices by JAX's collectives and lax.ppermute only.
A program may use at most 32 MiB of HBM per device.

```python
import jax
import jax.numpy as jnp
from jax import lax

O = 256
V = 1024
S = 1
NAUX = 1024


def strengthened(values, key, source, target, shards_of, factor):
    def block_of(axis_at):
        return (jnp.arange(values.shape[axis_at]) // (values.shape[axis_at] // shards_of)).reshape((-1,) + (1,) * (values.ndim - 1 - axis_at))

    first = jax.random.permutation(key, shards_of)[block_of(target)]
    second = (block_of(target) + shards_of // 2) % shards_of
    return jnp.where((block_of(source) == first) | (block_of(source) == second), factor * values, values)


def steps_of(stream_key, shape, shards, least, top_value):
    gain, own = 1.0, jax.random.fold_in(stream_key, 6)
    for axis_at, blocks in shards:
        draws = jnp.exp(jax.random.uniform(jax.random.fold_in(own, axis_at), (blocks,), jnp.float32, least / len(shards), top_value / len(shards)))
        gain = gain * jnp.repeat(draws, shape[axis_at] // blocks).reshape([-1 if axis == axis_at else 1 for axis in range(len(shape))])
    return gain


def bell_draw(rng, dims, width, limit, pieces=(), held_as=jnp.bfloat16):
    loudness = steps_of(rng, dims, pieces, -0.22, 0.18) if pieces else 1.0
    drawn = jax.random.normal(rng, dims, jnp.float32) * width * loudness
    return jnp.minimum(jnp.maximum(drawn, -limit), limit).astype(held_as)


def bell_draw_with(stream_key, dims, width, reach, shards, heavy, held_as=jnp.bfloat16):
    values = width * jax.random.normal(stream_key, dims, jnp.float32)
    if shards:
        values = values * steps_of(stream_key, dims, shards, -0.22, 0.18)
    return jnp.clip(strengthened(values, jax.random.fold_in(stream_key, 3), *heavy), -reach, reach).astype(held_as)


def setup_inputs(seed: int = 0) -> dict:
    key_list = jax.random.split(jax.random.key(seed), 5)
    return {
        "pair_integrals": bell_draw(key_list[0], (O * O, NAUX), (O * NAUX) ** -0.5, 0.01171875, ((0, 1024),)),
        "screening": bell_draw(key_list[1], (NAUX, NAUX), NAUX ** -0.5, 0.1875),
        "virtual_integrals": bell_draw_with(key_list[2], (NAUX, V, V), V ** -0.5, 0.75, ((0, 1024),), (0, 1, 1024, 6.0)),
        "trials": bell_draw(key_list[3], (S, O, V), 1.0, 6.0, ((2, 64),)),
    }


def reference(pair_integrals, screening, virtual_integrals, trials):
    screened = jnp.dot(pair_integrals, screening, preferred_element_type=jnp.float32).astype(jnp.bfloat16)
    trial_rows = trials.astype(jnp.float32).reshape(S * O, V)

    def add_aux(running, inputs):
        slab, column = inputs
        halves = jnp.dot(slab.astype(jnp.float32), trial_rows.T, preferred_element_type=jnp.float32)
        halves = lax.optimization_barrier(halves.astype(jnp.bfloat16)).astype(jnp.float32).reshape(V, S, O)
        tiles = column.astype(jnp.float32).reshape(O, O)
        return running + jnp.einsum("asj,ij->asi", halves, tiles), None

    zeroes = jnp.zeros((V, S, O), jnp.float32)
    response, unused = lax.scan(add_aux, zeroes, (virtual_integrals, screened.T))
    return response
```

```python
import jax
import jax.numpy as jnp
from jax import lax
from jax.experimental import pallas as pl
from jax.experimental.pallas import tpu as pltpu
from jax.sharding import PartitionSpec as P

O = 256
V = 1024
W = 16
N = 64
BLK = 16
BF = jnp.bfloat16
F32 = jnp.float32


def iota(shape, axis):
    return lax.broadcasted_iota(jnp.int32, shape, axis)


def picks(mask):
    return jnp.where(mask, 1.0, 0.0).astype(BF)


def dot(a, b, ca, cb):
    return lax.dot_general(a, b, (((ca,), (cb,)), ((), ())), preferred_element_type=F32)


def first_messages(wide_at, pairs, screening, trials):
    screened = dot(pairs, screening, 1, 0)
    columns = screened.T.astype(BF)
    tile_of = picks(iota((O, O), 0) == wide_at * BLK + iota((O, O), 1) // BLK)
    spread = dot(trials, tile_of, 1, 0)
    row = jnp.sum(jnp.where(iota((BLK, O), 0) == iota((BLK, O), 1) % BLK, spread, 0.0), 0, keepdims=True)
    parts = [columns[N * w : N * (w + 1), :] for w in range(W)]
    return jnp.concatenate(parts + [jnp.broadcast_to(row, (N, O)).astype(BF)], 1)


def second_messages(got):
    order = picks(iota((N, N), 1) == (iota((N, N), 0) % BLK) * 4 + iota((N, N), 0) // BLK)
    tiles = dot(order, got[:, :V], 1, 0)
    left = iota((BLK, 128), 1) < 64
    blocks = []
    for k in range(W // 2):
        t = [tiles[BLK * j : BLK * (j + 1), 128 * k : 128 * (k + 1)] for j in range(4)]
        r = [pltpu.roll(u, 64, 1) for u in t]
        even = [jnp.where(left, t[0], r[1]), jnp.where(left, t[2], r[3])]
        odd = [jnp.where(left, r[0], t[1]), jnp.where(left, r[2], t[3])]
        blocks += [jnp.concatenate(even, 1).astype(BF), jnp.concatenate(odd, 1).astype(BF)]
    rows = dot(picks(iota((V, N), 0) // BLK == iota((V, N), 1)), got[:, V:], 1, 0)
    kept = jnp.where(iota((V, O), 0) % BLK == iota((V, O), 1) % BLK, rows, 0.0).astype(BF)
    trials = dot(picks(iota((BLK, O), 0) == iota((BLK, O), 1) // BLK), kept, 1, 1).astype(BF)
    return blocks, trials


def third_messages(got):
    total = jnp.sum(got.astype(F32), 0).astype(BF)
    rows = dot(total, picks(iota((BLK, O), 0) == iota((BLK, O), 1) % BLK), 0, 0)
    kept = jnp.where(iota((V, O), 0) % BLK == iota((V, O), 1) // BLK, rows, 0.0).astype(BF)
    return dot(picks(iota((N, V), 0) == iota((N, V), 1) // BLK), kept, 1, 0).astype(BF)


def last_sum(got):
    total = jnp.sum(got.astype(F32), 0, keepdims=True)
    rows = jnp.where(iota((BLK, O), 0) == iota((BLK, O), 1) // BLK, total, 0.0)
    lanes = jnp.where(iota((O, BLK), 0) % BLK == iota((O, BLK), 1), 1.0, 0.0)
    return lax.dot_general(
        rows, lanes, (((1,), (0,)), ((), ())), precision=lax.Precision.HIGHEST, preferred_element_type=F32
    )


def store_pairs(ref, rows):
    half = rows.shape[1] // 2
    ref[:, 0, :] = rows[:, :half]
    ref[:, 1, :] = rows[:, half:]


def load_pairs(ref):
    return jnp.concatenate([ref[:, 0, :], ref[:, 1, :]], 1)


def first_kernel(wide_ref, pairs_ref, screening_ref, trials_ref, out_ref):
    store_pairs(out_ref, first_messages(wide_ref[0], pairs_ref[...], screening_ref[...], trials_ref[...]))


def second_kernel(got_ref, out_ref):
    blocks, trials = second_messages(load_pairs(got_ref))
    for w in range(W):
        out_ref[w, :, :O] = blocks[w]
        out_ref[w, :, O:] = trials


def third_kernel(got_ref, out_ref):
    store_pairs(out_ref, third_messages(got_ref[...]))


def last_kernel(got_ref, out_ref):
    out_ref[...] = last_sum(load_pairs(got_ref)).reshape(BLK, 1, BLK)


def call(body, shape, dtype, *args):
    specs = [pl.BlockSpec(memory_space=pltpu.VMEM)] * len(args)
    if args[0].dtype == jnp.int32:
        specs[0] = pl.BlockSpec(memory_space=pltpu.SMEM)
    return pl.pallas_call(
        body,
        out_shape=jax.ShapeDtypeStruct(shape, dtype),
        in_specs=specs,
        out_specs=pl.BlockSpec(memory_space=pltpu.VMEM),
        name=body.__name__,
    )(*args)


def swap(v, axis):
    return lax.all_to_all(v, axis, 0, 0, tiled=True)


def per_device(pair_integrals, screening, virtual_integrals, trials):
    wide_at = lax.axis_index("wide").reshape(1).astype(jnp.int32)
    mine = trials.reshape(O, BLK).T
    got = swap(call(first_kernel, (N, 2, (V + O) // 2), BF, wide_at, pair_integrals, screening, mine), "narrow")
    got = swap(call(second_kernel, (W, BLK, O + V), BF, got), "wide").reshape(O, O + V)
    halves = dot(virtual_integrals.reshape(V, V), got[:, O:], 1, 1).astype(BF)
    partial = dot(got[:, :O], halves, 1, 1).astype(BF)
    got = swap(partial.reshape(W, BLK, V), "wide")
    got = swap(call(third_kernel, (N, 2, O // 2), BF, got), "narrow")
    return call(last_kernel, (BLK, 1, BLK), F32, got)


def solution(mesh):
    return jax.shard_map(
        per_device,
        mesh=mesh,
        in_specs=(
            P(("wide", "narrow"), None),
            P(),
            P(("wide", "narrow"), None, None),
            P(None, None, "narrow"),
        ),
        out_specs=P("narrow", None, "wide"),
        check_vma=False,
    )
```

```python
import jax
import jax.numpy as jnp
from jax import lax
from jax.experimental import pallas as pl
from jax.experimental.pallas import tpu as pltpu
from jax.sharding import PartitionSpec as P

O = 256
V = 1024
W = 16
N = 64
BLK = 16
BF = jnp.bfloat16
F32 = jnp.float32


def iota(shape, axis):
    return lax.broadcasted_iota(jnp.int32, shape, axis)


def picks(mask):
    return jnp.where(mask, 1.0, 0.0).astype(BF)


def dot(a, b, ca, cb):
    return lax.dot_general(a, b, (((ca,), (cb,)), ((), ())), preferred_element_type=F32)


def first_messages(wide_at, pairs, screening, trials):
    screened = dot(pairs, screening, 1, 0)
    columns = screened.T.astype(BF)
    tile_of = picks(iota((O, O), 0) == wide_at * BLK + iota((O, O), 1) // BLK)
    spread = dot(trials, tile_of, 1, 0)
    row = jnp.sum(jnp.where(iota((BLK, O), 0) == iota((BLK, O), 1) % BLK, spread, 0.0), 0, keepdims=True)
    parts = [columns[N * w : N * (w + 1), :] for w in range(W)]
    return jnp.concatenate(parts + [jnp.broadcast_to(row, (N, O)).astype(BF)], 1)


def second_messages(got):
    order = picks(iota((N, N), 1) == (iota((N, N), 0) % BLK) * 4 + iota((N, N), 0) // BLK)
    tiles = dot(order, got[:, :V], 1, 0)
    left = iota((BLK, 128), 1) < 64
    blocks = []
    for k in range(W // 2):
        t = [tiles[BLK * j : BLK * (j + 1), 128 * k : 128 * (k + 1)] for j in range(4)]
        r = [pltpu.roll(u, 64, 1) for u in t]
        even = [jnp.where(left, t[0], r[1]), jnp.where(left, t[2], r[3])]
        odd = [jnp.where(left, r[0], t[1]), jnp.where(left, r[2], t[3])]
        blocks += [jnp.concatenate(even, 1).astype(BF), jnp.concatenate(odd, 1).astype(BF)]
    rows = dot(picks(iota((V, N), 0) // BLK == iota((V, N), 1)), got[:, V:], 1, 0)
    kept = jnp.where(iota((V, O), 0) % BLK == iota((V, O), 1) % BLK, rows, 0.0).astype(BF)
    trials = dot(picks(iota((BLK, O), 0) == iota((BLK, O), 1) // BLK), kept, 1, 1).astype(BF)
    return blocks, trials


def third_messages(got):
    total = jnp.sum(got.astype(F32), 0).astype(BF)
    rows = dot(total, picks(iota((BLK, O), 0) == iota((BLK, O), 1) % BLK), 0, 0)
    kept = jnp.where(iota((V, O), 0) % BLK == iota((V, O), 1) // BLK, rows, 0.0).astype(BF)
    return dot(picks(iota((N, V), 0) == iota((N, V), 1) // BLK), kept, 1, 0).astype(BF)


def last_sum(got):
    total = jnp.sum(got.astype(F32), 0, keepdims=True)
    rows = jnp.where(iota((BLK, O), 0) == iota((BLK, O), 1) // BLK, total, 0.0)
    lanes = jnp.where(iota((O, BLK), 0) % BLK == iota((O, BLK), 1), 1.0, 0.0)
    return lax.dot_general(
        rows, lanes, (((1,), (0,)), ((), ())), precision=lax.Precision.HIGHEST, preferred_element_type=F32
    )


def store_pairs(ref, rows):
    half = rows.shape[1] // 2
    ref[:, 0, :] = rows[:, :half]
    ref[:, 1, :] = rows[:, half:]


def load_pairs(ref):
    return jnp.concatenate([ref[:, 0, :], ref[:, 1, :]], 1)


def first_kernel(wide_ref, pairs_ref, screening_ref, trials_ref, out_ref):
    store_pairs(out_ref, first_messages(wide_ref[0], pairs_ref[...], screening_ref[...], trials_ref[...]))


def second_kernel(got_ref, out_ref):
    blocks, trials = second_messages(load_pairs(got_ref))
    for w in range(W):
        out_ref[w, :, :O] = blocks[w]
        out_ref[w, :, O:] = trials


def third_kernel(got_ref, out_ref):
    store_pairs(out_ref, third_messages(got_ref[...]))


def last_kernel(got_ref, out_ref):
    out_ref[...] = last_sum(load_pairs(got_ref)).reshape(BLK, 1, BLK)


def in_vmem(v):
    return pltpu.with_memory_space_constraint(v, pltpu.VMEM)


def call(body, shape, dtype, *args):
    specs = [pl.BlockSpec(memory_space=pltpu.VMEM)] * len(args)
    if args[0].dtype == jnp.int32:
        specs[0] = pl.BlockSpec(memory_space=pltpu.SMEM)
    return pl.pallas_call(
        body,
        out_shape=pltpu.VMEM(shape, dtype) if body is not last_kernel else jax.ShapeDtypeStruct(shape, dtype),
        in_specs=specs,
        out_specs=pl.BlockSpec(memory_space=pltpu.VMEM),
        name=body.__name__,
    )(*[in_vmem(a) if body is not first_kernel else a for a in args])


def swap(v, axis):
    return lax.all_to_all(v, axis, 0, 0, tiled=True)


def per_device(pair_integrals, screening, virtual_integrals, trials):
    wide_at = lax.axis_index("wide").reshape(1).astype(jnp.int32)
    mine = trials.reshape(O, BLK).T
    got = swap(call(first_kernel, (N, 2, (V + O) // 2), BF, wide_at, pair_integrals, screening, mine), "narrow")
    got = swap(call(second_kernel, (W, BLK, O + V), BF, got), "wide").reshape(O, O + V)
    halves = dot(virtual_integrals.reshape(V, V), got[:, O:], 1, 1).astype(BF)
    partial = dot(got[:, :O], halves, 1, 1).astype(BF)
    got = swap(partial.reshape(W, BLK, V), "wide")
    got = swap(call(third_kernel, (N, 2, O // 2), BF, got), "narrow")
    return call(last_kernel, (BLK, 1, BLK), F32, got)


def solution(mesh):
    return jax.shard_map(
        per_device,
        mesh=mesh,
        in_specs=(
            P(("wide", "narrow"), None),
            P(),
            P(("wide", "narrow"), None, None),
            P(None, None, "narrow"),
        ),
        out_specs=P("narrow", None, "wide"),
        check_vma=False,
    )
```

```python
import jax
import jax.numpy as jnp
from jax import lax
from jax.experimental import pallas as pl
from jax.experimental.pallas import tpu as pltpu
from jax.sharding import Mesh, PartitionSpec as P

O = 256
V = 1024
W = 16
Z = 16
BLK = 16
XY = ("xh", "y", "xl")
ALL = ("xh", "y", "z", "xl", "c")
BF = jnp.bfloat16
F32 = jnp.float32


def iota(shape, axis):
    return lax.broadcasted_iota(jnp.int32, shape, axis)


def ones_at(mask, dtype=BF):
    return jnp.where(mask, 1.0, 0.0).astype(dtype)


def dot(a, b, ca, cb, precision=None):
    return lax.dot_general(
        a, b, (((ca,), (cb,)), ((), ())), precision=precision, preferred_element_type=F32
    )


def first_kernel(at_ref, pairs_ref, screening_ref, trials_ref, out_ref, columns_ref):
    columns_ref[...] = dot(pairs_ref[...], screening_ref[...], 1, 0).T
    mine = iota((BLK, O), 0) == at_ref[0]
    row = jnp.sum(jnp.where(mine, trials_ref[...].astype(F32), 0.0), 0, keepdims=True)
    rank = iota((8, 128), 0)
    tail = jnp.where(rank == 0, row[:, :128], jnp.where(rank == 1, row[:, 128:], 0.0)).astype(BF)
    for z in range(Z):
        for x in range(2):
            left, right = (columns_ref[pl.ds(4 * z + 2 * x + c, W, 64), :] for c in range(2))
            out_ref[z, W * x : W * (x + 1), :] = jnp.concatenate([left, right], 1).astype(BF)
        out_ref[z, 32:, :] = tail


def second_kernel(got_ref, out_ref, rows_ref):
    rows_ref[...] = got_ref[...].reshape(Z * 40, 128).astype(F32)
    trials = jnp.concatenate([rows_ref[pl.ds(r, Z, 40), :] for r in (32, 33)], 1).astype(BF)
    for w in range(W):
        for x in range(2):
            out_ref[2 * w + x, :, :128] = rows_ref[pl.ds(W * x + w, Z, 40), :].astype(BF)
            out_ref[2 * w + x, :, 128:] = trials


def third_kernel(at_ref, own_ref, other_ref, virtual_ref, send_ref, keep_ref, screened_ref, trials_ref):
    core = at_ref[0]
    here = iota((BLK, 128), 1) // 64 == core
    for w in range(W):
        for x in range(2):
            moved = pltpu.roll(other_ref[2 * w + x, :, :128].astype(F32), 64, 1)
            tile = jnp.where(here, own_ref[2 * w + x, :, :128].astype(F32), moved)
            screened_ref[BLK * w : BLK * (w + 1), 128 * x : 128 * (x + 1)] = tile.astype(BF)
    flip = ones_at(iota((O, O), 1) == iota((O, O), 0) % W * Z + iota((O, O), 0) // W)
    for x in range(2):
        for ref, c in ((own_ref, core), (other_ref, 1 - core)):
            tile = jnp.concatenate([ref[2 * w + x, :, 128:] for w in range(W)], 0)
            tile = dot(flip, tile, 1, 0).astype(BF)
            for z in range(Z):
                start = pl.multiple_of(64 * z + 32 * x + BLK * c, BLK)
                trials_ref[pl.ds(start, BLK), :] = tile[W * z : W * (z + 1), :]
    for ref, c in ((send_ref, 1 - core), (keep_ref, core)):
        for x in range(2):
            rows = virtual_ref[:, 2 * x + c].reshape(O, V)
            halves = dot(rows, trials_ref[...], 1, 0).astype(BF)
            part = dot(screened_ref[...], halves, 1, 1).astype(ref.dtype)
            for w in range(W):
                ref[2 * w + x] = part[BLK * w : BLK * (w + 1), :]


def add_kernel(kept_ref, got_ref, out_ref):
    out_ref[...] = (kept_ref[...] + got_ref[...].astype(F32)).astype(BF)


def fourth_kernel(got_ref, out_ref):
    total = jnp.sum(got_ref[...].astype(F32), 0)
    full = lax.Precision.HIGHEST
    rows = dot(total, ones_at(iota((BLK, O), 0) == iota((BLK, O), 1) % BLK, F32), 0, 0, full)
    kept = jnp.where(iota((O, O), 0) % BLK == iota((O, O), 1) // BLK, rows, 0.0)
    tiles = dot(ones_at(iota((Z, O), 0) == iota((Z, O), 1) // BLK, F32), kept, 1, 0, full)
    out_ref[:, 0, :] = tiles[:, :128]
    out_ref[:, 1, :] = tiles[:, 128:]


def last_kernel(got_ref, out_ref):
    total = jnp.sum(jnp.concatenate([got_ref[:, 0, :], got_ref[:, 1, :]], 1), 0, keepdims=True)
    rows = jnp.where(iota((BLK, O), 0) == iota((BLK, O), 1) // BLK, total, 0.0)
    lanes = ones_at(iota((O, BLK), 0) % BLK == iota((O, BLK), 1), F32)
    out_ref[...] = dot(rows, lanes, 1, 0, lax.Precision.HIGHEST).reshape(BLK, 1, BLK)


def in_vmem(v):
    return pltpu.with_memory_space_constraint(v, pltpu.VMEM)


def vmem_out(shape, dtype):
    return pltpu.VMEM(shape, dtype)


def call(body, outs, *args, scratch=(), limit=24 << 20):
    vmem = pl.BlockSpec(memory_space=pltpu.VMEM)
    specs = [pl.BlockSpec(memory_space=pltpu.SMEM) if a.dtype == jnp.int32 else vmem for a in args]
    return pl.pallas_call(
        body,
        out_shape=outs,
        in_specs=specs,
        out_specs=jax.tree.map(lambda o: vmem, outs),
        scratch_shapes=scratch,
        compiler_params=pltpu.CompilerParams(vmem_limit_bytes=limit),
        name=body.__name__,
    )(*args)


def swap(v, axis):
    return in_vmem(lax.all_to_all(v, axis, 0, 0, tiled=True))


def across(v):
    return in_vmem(lax.ppermute(v, "c", [(0, 1), (1, 0)]))


def per_device(pair_integrals, screening, virtual_integrals, trials):
    at = lax.axis_index(("xh", "y")).reshape(1).astype(jnp.int32)
    core = lax.axis_index("c").reshape(1).astype(jnp.int32)
    sent = call(
        first_kernel,
        vmem_out((Z, 40, 128), BF),
        at,
        pair_integrals,
        screening,
        trials.reshape(O, BLK).T,
        scratch=[pltpu.VMEM((V, 64), F32)],
        limit=None,
    )
    got = swap(sent, "z")
    sent = call(second_kernel, vmem_out((2 * W, Z, 384), BF), got, scratch=[pltpu.VMEM((Z * 40, 128), F32)])
    own = swap(sent, XY)
    sent, kept = call(
        third_kernel,
        (vmem_out((2 * W, BLK, O), BF), vmem_out((2 * W, BLK, O), F32)),
        core,
        own,
        across(own),
        in_vmem(virtual_integrals.reshape(Z, 4, BLK, V)),
        scratch=[pltpu.VMEM((O, O), BF), pltpu.VMEM((V, O), BF)],
    )
    got = swap(call(add_kernel, vmem_out((2 * W, BLK, O), BF), kept, across(sent)), XY)
    got = swap(call(fourth_kernel, vmem_out((Z, 2, 128), F32), got), "z")
    return call(last_kernel, jax.ShapeDtypeStruct((BLK, 1, BLK), F32), got)


def solution(mesh):
    chips = Mesh(mesh.devices.reshape(2, 8, 16, 2, 2), ALL)
    return jax.shard_map(
        per_device,
        mesh=chips,
        in_specs=(
            P(ALL, None),
            P(),
            P(ALL, None, None),
            P(None, None, ("z", "xl", "c")),
        ),
        out_specs=P(("z", "xl", "c"), None, ("xh", "y")),
        check_vma=False,
    )
```

```python
import jax
import jax.numpy as jnp
from jax import lax
from jax.experimental import pallas as pl
from jax.experimental.pallas import tpu as pltpu
from jax.sharding import Mesh, PartitionSpec as P

O = 256
V = 1024
W = 16
Z = 16
BLK = 16
XY = ("xh", "y", "xl")
ALL = ("xh", "y", "z", "xl", "c")
BF = jnp.bfloat16
F32 = jnp.float32


def iota(shape, axis):
    return lax.broadcasted_iota(jnp.int32, shape, axis)


def ones_at(mask, dtype=BF):
    return jnp.where(mask, 1.0, 0.0).astype(dtype)


def dot(a, b, ca, cb, precision=None):
    return lax.dot_general(
        a, b, (((ca,), (cb,)), ((), ())), precision=precision, preferred_element_type=F32
    )


def first_kernel(
    at_ref, pairs_hbm, screening_hbm, trials_hbm, out_ref, pairs_ref, screening_ref, trials_ref, columns_ref, sems
):
    copies = [pltpu.make_async_copy(pairs_hbm, pairs_ref, sems.at[0])]
    for k in range(4):
        part = pl.ds(256 * k, 256)
        copies.append(pltpu.make_async_copy(screening_hbm.at[:, part], screening_ref.at[:, part], sems.at[1 + k]))
    copies.append(pltpu.make_async_copy(trials_hbm, trials_ref, sems.at[5]))
    for copy in copies:
        copy.start()
    copies[0].wait()
    for k in range(4):
        copies[1 + k].wait()
        part = slice(256 * k, 256 * (k + 1))
        columns_ref[part, :] = dot(pairs_ref[...], screening_ref[:, part], 1, 0).T
    copies[5].wait()
    mine = iota((BLK, O), 0) == at_ref[0]
    row = jnp.sum(jnp.where(mine, trials_ref[...].astype(F32), 0.0), 0, keepdims=True)
    rank = iota((8, 128), 0)
    tail = jnp.where(rank == 0, row[:, :128], jnp.where(rank == 1, row[:, 128:], 0.0)).astype(BF)
    for z in range(Z):
        for x in range(2):
            left, right = (columns_ref[pl.ds(4 * z + 2 * x + c, W, 64), :] for c in range(2))
            out_ref[z, W * x : W * (x + 1), :] = jnp.concatenate([left, right], 1).astype(BF)
        out_ref[z, 32:, :] = tail


def second_kernel(got_ref, out_ref, rows_ref):
    rows_ref[...] = got_ref[...].reshape(Z * 40, 128).astype(F32)
    trials = jnp.concatenate([rows_ref[pl.ds(r, Z, 40), :] for r in (32, 33)], 1).astype(BF)
    for w in range(W):
        for x in range(2):
            out_ref[2 * w + x, :, :128] = rows_ref[pl.ds(W * x + w, Z, 40), :].astype(BF)
            out_ref[2 * w + x, :, 128:] = trials


def ordered(ref):
    flip = ones_at(iota((O, O), 1) == iota((O, O), 0) % W * Z + iota((O, O), 0) // W)
    tiles = [jnp.concatenate([ref[2 * w + x, :, 128:] for w in range(W)], 0) for x in range(2)]
    return [dot(flip, tile, 1, 0).astype(BF) for tile in tiles]


def own_kernel(own_ref, trials_ref):
    trials_ref[0], trials_ref[1] = ordered(own_ref)


def partial(of, screened_ref, trials_ref, virtual_ref, out_ref):
    for x in range(2):
        rows = virtual_ref[:, 2 * x + of].reshape(O, V)
        halves = dot(rows, trials_ref[...], 1, 0).astype(BF)
        part = dot(screened_ref[...], halves, 1, 1).astype(out_ref.dtype)
        for w in range(W):
            out_ref[2 * w + x] = part[BLK * w : BLK * (w + 1), :]


def send_kernel(at_ref, own_ref, own_trials_ref, other_ref, virtual_ref, send_ref, screened_ref, trials_ref):
    core = at_ref[0]
    here = iota((BLK, 128), 1) // 64 == core
    for w in range(W):
        for x in range(2):
            moved = pltpu.roll(other_ref[2 * w + x, :, :128].astype(F32), 64, 1)
            tile = jnp.where(here, own_ref[2 * w + x, :, :128].astype(F32), moved)
            screened_ref[BLK * w : BLK * (w + 1), 128 * x : 128 * (x + 1)] = tile.astype(BF)
    for tiles, c in (((own_trials_ref[0], own_trials_ref[1]), core), (ordered(other_ref), 1 - core)):
        for x in range(2):
            for z in range(Z):
                start = pl.multiple_of(64 * z + 32 * x + BLK * c, BLK)
                trials_ref[pl.ds(start, BLK), :] = tiles[x][W * z : W * (z + 1), :]
    partial(1 - core, screened_ref, trials_ref, virtual_ref, send_ref)


def keep_kernel(at_ref, screened_ref, trials_ref, virtual_ref, keep_ref):
    partial(at_ref[0], screened_ref, trials_ref, virtual_ref, keep_ref)


def add_kernel(kept_ref, got_ref, out_ref):
    out_ref[...] = (kept_ref[...] + got_ref[...].astype(F32)).astype(BF)


def fourth_kernel(got_ref, out_ref):
    total = jnp.sum(got_ref[...].astype(F32), 0)
    row, chunk = iota((8, 128), 0), iota((8, 128), 1) // BLK
    for r in range(2):
        for h in range(2):
            t = total[8 * r : 8 * (r + 1), 128 * h : 128 * (h + 1)]
            for s in (1, 2, 4):
                up = pltpu.roll(pltpu.roll(t, 8 - s, 0), BLK * s, 1)
                down = pltpu.roll(pltpu.roll(t, s, 0), 128 - BLK * s, 1)
                high, right = row & s != 0, chunk & s != 0
                t = jnp.where(high == right, t, jnp.where(right, up, down))
            out_ref[8 * h : 8 * (h + 1), r, :] = t


def last_kernel(got_ref, out_ref):
    rows = []
    for r in range(2):
        total = jnp.sum(got_ref[:, r, :], 0, keepdims=True)
        t = jnp.where(iota((8, 128), 0) == iota((8, 128), 1) // BLK, total, 0.0)
        for s in (64, 32, BLK):
            t = t + pltpu.roll(t, s, 1)
        rows.append(t)
    out_ref[...] = jnp.concatenate(rows, 0).T[:BLK, :].reshape(BLK, 1, BLK)


def in_vmem(v):
    return pltpu.with_memory_space_constraint(v, pltpu.VMEM)


def in_hbm(v):
    return pltpu.with_memory_space_constraint(v, pltpu.HBM)


def vmem_out(shape, dtype):
    return pltpu.VMEM(shape, dtype)


def call(body, outs, *args, scratch=(), limit=24 << 20, hbm=False):
    vmem = pl.BlockSpec(memory_space=pltpu.VMEM)
    space = pl.BlockSpec(memory_space=pltpu.HBM) if hbm else vmem
    specs = [pl.BlockSpec(memory_space=pltpu.SMEM) if a.dtype == jnp.int32 else space for a in args]
    return pl.pallas_call(
        body,
        out_shape=outs,
        in_specs=specs,
        out_specs=jax.tree.map(lambda o: vmem, outs),
        scratch_shapes=scratch,
        compiler_params=pltpu.CompilerParams(vmem_limit_bytes=limit),
        name=body.__name__,
    )(*args)


def swap(v, axis):
    return in_vmem(lax.all_to_all(v, axis, 0, 0, tiled=True))


def across(v):
    return in_vmem(lax.ppermute(v, "c", [(0, 1), (1, 0)]))


def per_device(pair_integrals, screening, virtual_integrals, trials):
    at = lax.axis_index(("xh", "y")).reshape(1).astype(jnp.int32)
    core = lax.axis_index("c").reshape(1).astype(jnp.int32)
    sent = call(
        first_kernel,
        vmem_out((Z, 40, 128), BF),
        at,
        in_hbm(pair_integrals),
        in_hbm(screening),
        in_hbm(trials.reshape(O, BLK).T),
        scratch=[
            pltpu.VMEM((64, V), BF),
            pltpu.VMEM((V, V), BF),
            pltpu.VMEM((BLK, O), BF),
            pltpu.VMEM((V, 64), F32),
            pltpu.SemaphoreType.DMA((6,)),
        ],
        hbm=True,
    )
    got = swap(sent, "z")
    sent = call(second_kernel, vmem_out((2 * W, Z, 384), BF), got, scratch=[pltpu.VMEM((Z * 40, 128), F32)])
    own = swap(sent, XY)
    other = across(own)
    own_trials = call(own_kernel, vmem_out((2, O, O), BF), own)
    virtual = in_vmem(virtual_integrals.reshape(Z, 4, BLK, V))
    sent, screened, whole = call(
        send_kernel,
        (vmem_out((2 * W, BLK, O), BF), vmem_out((O, O), BF), vmem_out((V, O), BF)),
        core,
        own,
        own_trials,
        other,
        virtual,
    )
    got = across(sent)
    kept = call(keep_kernel, vmem_out((2 * W, BLK, O), F32), core, screened, whole, virtual)
    got = swap(call(add_kernel, vmem_out((2 * W, BLK, O), BF), kept, got), XY)
    got = swap(call(fourth_kernel, vmem_out((Z, 2, 128), F32), got), "z")
    return call(last_kernel, jax.ShapeDtypeStruct((BLK, 1, BLK), F32), got)


def solution(mesh):
    chips = Mesh(mesh.devices.reshape(2, 8, 16, 2, 2), ALL)
    return jax.shard_map(
        per_device,
        mesh=chips,
        in_specs=(
            P(ALL, None),
            P(),
            P(ALL, None, None),
            P(None, None, ("z", "xl", "c")),
        ),
        out_specs=P(("z", "xl", "c"), None, ("xh", "y")),
        check_vma=False,
    )
```

```python
import jax
import jax.numpy as jnp
from jax import lax
from jax.experimental import pallas as pl
from jax.experimental.pallas import tpu as pltpu
from jax.sharding import Mesh, PartitionSpec as P

O = 256
V = 1024
W = 16
Z = 16
BLK = 16
STEP = 72
XY = ("xh", "y", "xl")
ALL = ("xh", "y", "z", "xl", "c")
BF = jnp.bfloat16
F32 = jnp.float32


def iota(shape, axis):
    return lax.broadcasted_iota(jnp.int32, shape, axis)


def ones_at(mask, dtype=BF):
    return jnp.where(mask, 1.0, 0.0).astype(dtype)


def dot(a, b, ca, cb, precision=None):
    return lax.dot_general(
        a, b, (((ca,), (cb,)), ((), ())), precision=precision, preferred_element_type=F32
    )


def first_kernel(
    at_ref, pairs_hbm, screening_hbm, trials_hbm, out_ref, pairs_ref, screening_ref, trials_ref, columns_ref, sems
):
    copies = [pltpu.make_async_copy(pairs_hbm, pairs_ref, sems.at[0])]
    for k in range(2):
        part = pl.ds(O * 2 * k, O * 2)
        copies.append(pltpu.make_async_copy(screening_hbm.at[:, part], screening_ref.at[:, part], sems.at[1 + k]))
    copies.append(pltpu.make_async_copy(trials_hbm, trials_ref, sems.at[3]))
    for copy in copies:
        copy.start()
    copies[0].wait()
    for k in range(2):
        copies[1 + k].wait()
        columns = dot(pairs_ref[...], screening_ref[:, O * 2 * k : O * 2 * (k + 1)], 1, 0).T
        for w in range(8):
            columns_ref[pl.ds(STEP * (8 * k + w), 64), :] = columns[64 * w : 64 * (w + 1), :]
    copies[3].wait()
    mine = iota((BLK, O), 0) == at_ref[0]
    row = jnp.sum(jnp.where(mine, trials_ref[...].astype(F32), 0.0), 0, keepdims=True)
    rank = iota((8, 128), 0)
    tail = jnp.where(rank == 0, row[:, :128], jnp.where(rank == 1, row[:, 128:], 0.0)).astype(BF)
    for z in range(Z):
        for x in range(2):
            left, right = (columns_ref[pl.ds(4 * z + 2 * x + c, W, STEP), :] for c in range(2))
            out_ref[z, W * x : W * (x + 1), :] = jnp.concatenate([left, right], 1).astype(BF)
        out_ref[z, 32:, :] = tail


def second_kernel(got_ref, out_ref, rows_ref):
    rows_ref[...] = got_ref[...].reshape(Z * 40, 128).astype(F32)
    trials = jnp.concatenate([rows_ref[pl.ds(r, Z, 40), :] for r in (32, 33)], 1).astype(BF)
    for w in range(W):
        for x in range(2):
            out_ref[2 * w + x, :, :128] = rows_ref[pl.ds(W * x + w, Z, 40), :].astype(BF)
            out_ref[2 * w + x, :, 128:] = trials


def ordered(ref):
    flip = ones_at(iota((O, O), 1) == iota((O, O), 0) % W * Z + iota((O, O), 0) // W)
    tiles = [jnp.concatenate([ref[2 * w + x, :, 128:] for w in range(W)], 0) for x in range(2)]
    return [dot(flip, tile, 1, 0).astype(BF) for tile in tiles]


def own_kernel(own_ref, trials_ref):
    trials_ref[0], trials_ref[1] = ordered(own_ref)


def partial(of, screened_ref, trials_ref, virtual_ref, out_ref):
    for x in range(2):
        rows = virtual_ref[:, 2 * x + of].reshape(O, V)
        halves = dot(rows, trials_ref[...], 1, 0).astype(BF)
        part = dot(screened_ref[...], halves, 1, 1).astype(out_ref.dtype)
        for w in range(W):
            out_ref[2 * w + x] = part[BLK * w : BLK * (w + 1), :]


def send_kernel(at_ref, own_ref, own_trials_ref, other_ref, virtual_ref, send_ref, screened_ref, trials_ref):
    core = at_ref[0]
    here = iota((BLK, 128), 1) // 64 == core
    for w in range(W):
        for x in range(2):
            moved = pltpu.roll(other_ref[2 * w + x, :, :128].astype(F32), 64, 1)
            tile = jnp.where(here, own_ref[2 * w + x, :, :128].astype(F32), moved)
            screened_ref[BLK * w : BLK * (w + 1), 128 * x : 128 * (x + 1)] = tile.astype(BF)
    for tiles, c in (((own_trials_ref[0], own_trials_ref[1]), core), (ordered(other_ref), 1 - core)):
        for x in range(2):
            for z in range(Z):
                start = pl.multiple_of(64 * z + 32 * x + BLK * c, BLK)
                trials_ref[pl.ds(start, BLK), :] = tiles[x][W * z : W * (z + 1), :]
    partial(1 - core, screened_ref, trials_ref, virtual_ref, send_ref)


def keep_kernel(at_ref, screened_ref, trials_ref, virtual_ref, keep_ref):
    partial(at_ref[0], screened_ref, trials_ref, virtual_ref, keep_ref)


def add_kernel(kept_ref, got_ref, out_ref):
    out_ref[...] = (kept_ref[...] + got_ref[...].astype(F32)).astype(BF)


def fourth_kernel(got_ref, out_ref):
    total = jnp.sum(got_ref[...].astype(F32), 0)
    row, chunk = iota((8, 128), 0), iota((8, 128), 1) // BLK
    for r in range(2):
        for h in range(2):
            t = total[8 * r : 8 * (r + 1), 128 * h : 128 * (h + 1)]
            for s in (1, 2, 4):
                up = pltpu.roll(pltpu.roll(t, 8 - s, 0), BLK * s, 1)
                down = pltpu.roll(pltpu.roll(t, s, 0), 128 - BLK * s, 1)
                high, right = row & s != 0, chunk & s != 0
                t = jnp.where(high == right, t, jnp.where(right, up, down))
            out_ref[8 * h : 8 * (h + 1), r, :] = t


def last_kernel(got_ref, out_ref):
    rows = []
    for r in range(2):
        total = jnp.sum(got_ref[:, r, :], 0, keepdims=True)
        t = jnp.where(iota((8, 128), 0) == iota((8, 128), 1) // BLK, total, 0.0)
        for s in (64, 32, BLK):
            t = t + pltpu.roll(t, s, 1)
        rows.append(t)
    out_ref[...] = jnp.concatenate(rows, 0).T[:BLK, :].reshape(BLK, 1, BLK)


def in_vmem(v):
    return pltpu.with_memory_space_constraint(v, pltpu.VMEM)


def in_hbm(v):
    return pltpu.with_memory_space_constraint(v, pltpu.HBM)


def vmem_out(shape, dtype):
    return pltpu.VMEM(shape, dtype)


def call(body, outs, *args, scratch=(), limit=24 << 20, hbm=False):
    vmem = pl.BlockSpec(memory_space=pltpu.VMEM)
    space = pl.BlockSpec(memory_space=pltpu.HBM) if hbm else vmem
    specs = [pl.BlockSpec(memory_space=pltpu.SMEM) if a.dtype == jnp.int32 else space for a in args]
    return pl.pallas_call(
        body,
        out_shape=outs,
        in_specs=specs,
        out_specs=jax.tree.map(lambda o: vmem, outs),
        scratch_shapes=scratch,
        compiler_params=pltpu.CompilerParams(vmem_limit_bytes=limit),
        name=body.__name__,
    )(*args)


def swap(v, axis):
    return in_vmem(lax.all_to_all(v, axis, 0, 0, tiled=True))


def across(v):
    return in_vmem(lax.ppermute(v, "c", [(0, 1), (1, 0)]))


def per_device(pair_integrals, screening, virtual_integrals, trials):
    at = lax.axis_index(("xh", "y")).reshape(1).astype(jnp.int32)
    core = lax.axis_index("c").reshape(1).astype(jnp.int32)
    sent = call(
        first_kernel,
        vmem_out((Z, 40, 128), BF),
        at,
        in_hbm(pair_integrals),
        in_hbm(screening),
        in_hbm(trials.reshape(O, BLK).T),
        scratch=[
            pltpu.VMEM((64, V), BF),
            pltpu.VMEM((V, V), BF),
            pltpu.VMEM((BLK, O), BF),
            pltpu.VMEM((W * STEP, 64), F32),
            pltpu.SemaphoreType.DMA((4,)),
        ],
        hbm=True,
    )
    got = swap(sent, "z")
    sent = call(second_kernel, vmem_out((2 * W, Z, 384), BF), got, scratch=[pltpu.VMEM((Z * 40, 128), F32)])
    own = swap(sent, XY)
    other = across(own)
    own_trials = call(own_kernel, vmem_out((2, O, O), BF), own)
    virtual = in_vmem(virtual_integrals.reshape(Z, 4, BLK, V))
    sent, screened, whole = call(
        send_kernel,
        (vmem_out((2 * W, BLK, O), BF), vmem_out((O, O), BF), vmem_out((V, O), BF)),
        core,
        own,
        own_trials,
        other,
        virtual,
    )
    got = across(sent)
    kept = call(keep_kernel, vmem_out((2 * W, BLK, O), F32), core, screened, whole, virtual)
    got = swap(call(add_kernel, vmem_out((2 * W, BLK, O), BF), kept, got), XY)
    got = swap(call(fourth_kernel, vmem_out((Z, 2, 128), F32), got), "z")
    return call(last_kernel, jax.ShapeDtypeStruct((BLK, 1, BLK), F32), got)


def solution(mesh):
    chips = Mesh(mesh.devices.reshape(2, 8, 16, 2, 2), ALL)
    return jax.shard_map(
        per_device,
        mesh=chips,
        in_specs=(
            P(ALL, None),
            P(),
            P(ALL, None, None),
            P(None, None, ("z", "xl", "c")),
        ),
        out_specs=P(("z", "xl", "c"), None, ("xh", "y")),
        check_vma=False,
    )
```

```python
import jax
import jax.numpy as jnp
from jax import lax
from jax.experimental import pallas as pl
from jax.experimental.pallas import tpu as pltpu
from jax.sharding import Mesh, PartitionSpec as P

O = 256
V = 1024
W = 16
Z = 16
BLK = 16
STEP = 72
XY = ("xh", "y", "xl")
ALL = ("xh", "y", "z", "xl", "c")
BF = jnp.bfloat16
F32 = jnp.float32


def iota(shape, axis):
    return lax.broadcasted_iota(jnp.int32, shape, axis)


def ones_at(mask, dtype=BF):
    return jnp.where(mask, 1.0, 0.0).astype(dtype)


def dot(a, b, ca, cb, precision=None):
    return lax.dot_general(
        a, b, (((ca,), (cb,)), ((), ())), precision=precision, preferred_element_type=F32
    )


def first_kernel(
    at_ref, pairs_hbm, screening_hbm, trials_hbm, out_ref, pairs_ref, screening_ref, trials_ref, columns_ref, sems
):
    copies = [pltpu.make_async_copy(pairs_hbm, pairs_ref, sems.at[0])]
    for k in range(2):
        part = pl.ds(O * 2 * k, O * 2)
        copies.append(pltpu.make_async_copy(screening_hbm.at[:, part], screening_ref.at[:, part], sems.at[1 + k]))
    copies.append(pltpu.make_async_copy(trials_hbm, trials_ref, sems.at[3]))
    for copy in copies:
        copy.start()
    copies[0].wait()
    for k in range(2):
        copies[1 + k].wait()
        columns = dot(pairs_ref[...], screening_ref[:, O * 2 * k : O * 2 * (k + 1)], 1, 0).T
        for w in range(8):
            columns_ref[pl.ds(STEP * (8 * k + w), 64), :] = columns[64 * w : 64 * (w + 1), :]
    copies[3].wait()
    mine = iota((BLK, O), 0) == at_ref[0]
    row = jnp.sum(jnp.where(mine, trials_ref[...].astype(F32), 0.0), 0, keepdims=True)
    tail = jnp.where(iota((2, 128), 0) == 0, row[:, :128], row[:, 128:]).astype(BF)
    for z in range(Z):
        for x in range(2):
            left, right = (columns_ref[pl.ds(4 * z + 2 * x + c, W, STEP), :] for c in range(2))
            out_ref[z, 8 * x : 8 * (x + 1)] = jnp.concatenate([left, right], 1).astype(BF).reshape(8, 2, 128)
        out_ref[z, 16] = tail


def second_kernel(got_ref, out_ref, rows_ref):
    rows_ref[...] = got_ref[...].reshape(Z * 34, 128).astype(F32)
    trials = jnp.concatenate([rows_ref[pl.ds(r, Z, 34), :] for r in (32, 33)], 1).astype(BF)
    for w in range(W):
        for x in range(2):
            out_ref[2 * w + x, :, :128] = rows_ref[pl.ds(W * x + w, Z, 34), :].astype(BF)
            out_ref[2 * w + x, :, 128:] = trials


def ordered(ref):
    flip = ones_at(iota((O, O), 1) == iota((O, O), 0) % W * Z + iota((O, O), 0) // W)
    tiles = [jnp.concatenate([ref[2 * w + x, :, 128:] for w in range(W)], 0) for x in range(2)]
    return [dot(flip, tile, 1, 0).astype(BF) for tile in tiles]


def own_kernel(own_ref, virtual_hbm, trials_ref, virtual_ref, sem):
    copy = pltpu.make_async_copy(virtual_hbm, virtual_ref, sem)
    copy.start()
    trials_ref[0], trials_ref[1] = ordered(own_ref)
    copy.wait()


def partial(of, screened_ref, trials_ref, virtual_ref, out_ref):
    for x in range(2):
        rows = virtual_ref[:, 2 * x + of].reshape(O, V)
        halves = dot(rows, trials_ref[...], 1, 0).astype(BF)
        part = dot(screened_ref[...], halves, 1, 1).astype(out_ref.dtype)
        for w in range(W):
            out_ref[2 * w + x] = part[BLK * w : BLK * (w + 1), :]


def send_kernel(at_ref, own_ref, own_trials_ref, other_ref, virtual_ref, send_ref, screened_ref, trials_ref):
    core = at_ref[0]
    here = iota((BLK, 128), 1) // 64 == core
    for w in range(W):
        for x in range(2):
            moved = pltpu.roll(other_ref[2 * w + x, :, :128].astype(F32), 64, 1)
            tile = jnp.where(here, own_ref[2 * w + x, :, :128].astype(F32), moved)
            screened_ref[BLK * w : BLK * (w + 1), 128 * x : 128 * (x + 1)] = tile.astype(BF)
    for tiles, c in (((own_trials_ref[0], own_trials_ref[1]), core), (ordered(other_ref), 1 - core)):
        for x in range(2):
            for z in range(Z):
                start = pl.multiple_of(64 * z + 32 * x + BLK * c, BLK)
                trials_ref[pl.ds(start, BLK), :] = tiles[x][W * z : W * (z + 1), :]
    partial(1 - core, screened_ref, trials_ref, virtual_ref, send_ref)


def keep_kernel(at_ref, screened_ref, trials_ref, virtual_ref, keep_ref):
    partial(at_ref[0], screened_ref, trials_ref, virtual_ref, keep_ref)


def add_kernel(kept_ref, got_ref, out_ref):
    out_ref[...] = (kept_ref[...] + got_ref[...].astype(F32)).astype(BF)


def fourth_kernel(got_ref, out_ref):
    total = jnp.sum(got_ref[...].astype(F32), 0)
    row, chunk = iota((8, 128), 0), iota((8, 128), 1) // BLK
    for r in range(2):
        for h in range(2):
            t = total[8 * r : 8 * (r + 1), 128 * h : 128 * (h + 1)]
            for s in (1, 2, 4):
                up = pltpu.roll(pltpu.roll(t, 8 - s, 0), BLK * s, 1)
                down = pltpu.roll(pltpu.roll(t, s, 0), 128 - BLK * s, 1)
                high, right = row & s != 0, chunk & s != 0
                t = jnp.where(high == right, t, jnp.where(right, up, down))
            out_ref[8 * h : 8 * (h + 1), r, :] = t


def last_kernel(got_ref, out_ref):
    rows = []
    for r in range(2):
        total = jnp.sum(got_ref[:, r, :], 0, keepdims=True)
        t = jnp.where(iota((8, 128), 0) == iota((8, 128), 1) // BLK, total, 0.0)
        for s in (64, 32, BLK):
            t = t + pltpu.roll(t, s, 1)
        rows.append(t)
    out_ref[...] = jnp.concatenate(rows, 0).T[:BLK, :].reshape(BLK, 1, BLK)


def in_vmem(v):
    return pltpu.with_memory_space_constraint(v, pltpu.VMEM)


def in_hbm(v):
    return pltpu.with_memory_space_constraint(v, pltpu.HBM)


def vmem_out(shape, dtype):
    return pltpu.VMEM(shape, dtype)


def call(body, outs, *args, scratch=(), limit=24 << 20, hbm=()):
    vmem = pl.BlockSpec(memory_space=pltpu.VMEM)
    specs = [pl.BlockSpec(memory_space=pltpu.SMEM) if a.dtype == jnp.int32 else vmem for a in args]
    for at in hbm:
        specs[at] = pl.BlockSpec(memory_space=pltpu.HBM)
    return pl.pallas_call(
        body,
        out_shape=outs,
        in_specs=specs,
        out_specs=jax.tree.map(lambda o: vmem, outs),
        scratch_shapes=scratch,
        compiler_params=pltpu.CompilerParams(vmem_limit_bytes=limit),
        name=body.__name__,
    )(*args)


def swap(v, axis):
    return in_vmem(lax.all_to_all(v, axis, 0, 0, tiled=True))


def across(v):
    return in_vmem(lax.ppermute(v, "c", [(0, 1), (1, 0)]))


def per_device(pair_integrals, screening, virtual_integrals, trials):
    at = lax.axis_index(("xh", "y")).reshape(1).astype(jnp.int32)
    core = lax.axis_index("c").reshape(1).astype(jnp.int32)
    sent = call(
        first_kernel,
        vmem_out((Z, 17, 2, 128), BF),
        at,
        in_hbm(pair_integrals),
        in_hbm(screening),
        in_hbm(trials.reshape(O, BLK).T),
        scratch=[
            pltpu.VMEM((64, V), BF),
            pltpu.VMEM((V, V), BF),
            pltpu.VMEM((BLK, O), BF),
            pltpu.VMEM((W * STEP, 64), F32),
            pltpu.SemaphoreType.DMA((4,)),
        ],
        hbm=(1, 2, 3),
    )
    got = swap(sent, "z")
    sent = call(second_kernel, vmem_out((2 * W, Z, 384), BF), got, scratch=[pltpu.VMEM((Z * 34, 128), F32)])
    own = swap(sent, XY)
    other = across(own)
    own_trials, virtual = call(
        own_kernel,
        (vmem_out((2, O, O), BF), vmem_out((Z, 4, BLK, V), BF)),
        own,
        in_hbm(virtual_integrals.reshape(Z, 4, BLK, V)),
        scratch=[pltpu.SemaphoreType.DMA(())],
        hbm=(1,),
    )
    sent, screened, whole = call(
        send_kernel,
        (vmem_out((2 * W, BLK, O), BF), vmem_out((O, O), BF), vmem_out((V, O), BF)),
        core,
        own,
        own_trials,
        other,
        virtual,
    )
    got = across(sent)
    kept = call(keep_kernel, vmem_out((2 * W, BLK, O), F32), core, screened, whole, virtual)
    got = swap(call(add_kernel, vmem_out((2 * W, BLK, O), BF), kept, got), XY)
    got = swap(call(fourth_kernel, vmem_out((Z, 2, 128), F32), got), "z")
    return call(last_kernel, jax.ShapeDtypeStruct((BLK, 1, BLK), F32), got)


def solution(mesh):
    chips = Mesh(mesh.devices.reshape(2, 8, 16, 2, 2), ALL)
    return jax.shard_map(
        per_device,
        mesh=chips,
        in_specs=(
            P(ALL, None),
            P(),
            P(ALL, None, None),
            P(None, None, ("z", "xl", "c")),
        ),
        out_specs=P(("z", "xl", "c"), None, ("xh", "y")),
        check_vma=False,
    )
```

```python
import jax
import jax.numpy as jnp
from jax import lax
from jax.experimental import pallas as pl
from jax.experimental.pallas import tpu as pltpu
from jax.sharding import Mesh, PartitionSpec as P

O = 256
V = 1024
W = 16
Z = 16
BLK = 16
STEP = 72
XY = ("xh", "y", "xl")
ALL = ("xh", "y", "z", "xl", "c")
BF = jnp.bfloat16
F32 = jnp.float32


def iota(shape, axis):
    return lax.broadcasted_iota(jnp.int32, shape, axis)


def ones_at(mask, dtype=BF):
    return jnp.where(mask, 1.0, 0.0).astype(dtype)


def dot(a, b, ca, cb, precision=None):
    return lax.dot_general(
        a, b, (((ca,), (cb,)), ((), ())), precision=precision, preferred_element_type=F32
    )


def first_kernel(
    at_ref, pairs_hbm, screening_hbm, trials_hbm, out_ref, pairs_ref, screening_ref, trials_ref, columns_ref, sems
):
    copies = [pltpu.make_async_copy(pairs_hbm, pairs_ref, sems.at[0])]
    for k in range(8):
        part = (pl.ds(O * (k % 4), O), pl.ds(O * 2 * (k // 4), O * 2))
        copies.append(pltpu.make_async_copy(screening_hbm.at[part], screening_ref.at[part], sems.at[1 + k]))
    copies.append(pltpu.make_async_copy(trials_hbm, trials_ref, sems.at[9]))
    for copy in copies:
        copy.start()
    copies[0].wait()
    for k in range(2):
        for r in range(4):
            copies[1 + 4 * k + r].wait()
        columns = dot(pairs_ref[...], screening_ref[:, O * 2 * k : O * 2 * (k + 1)], 1, 0).T
        for w in range(8):
            columns_ref[pl.ds(STEP * (8 * k + w), 64), :] = columns[64 * w : 64 * (w + 1), :]
    copies[9].wait()
    mine = iota((BLK, O), 0) == at_ref[0]
    row = jnp.sum(jnp.where(mine, trials_ref[...].astype(F32), 0.0), 0, keepdims=True)
    tail = jnp.where(iota((2, 128), 0) == 0, row[:, :128], row[:, 128:]).astype(BF)
    for z in range(Z):
        for x in range(2):
            left, right = (columns_ref[pl.ds(4 * z + 2 * x + c, W, STEP), :] for c in range(2))
            out_ref[z, 8 * x : 8 * (x + 1)] = jnp.concatenate([left, right], 1).astype(BF).reshape(8, 2, 128)
        out_ref[z, 16] = tail


def second_kernel(got_ref, out_ref, rows_ref):
    rows_ref[...] = got_ref[...].reshape(Z * 34, 128).astype(F32)
    trials = jnp.concatenate([rows_ref[pl.ds(r, Z, 34), :] for r in (32, 33)], 1).astype(BF)
    for w in range(W):
        for x in range(2):
            out_ref[2 * w + x, :, :128] = rows_ref[pl.ds(W * x + w, Z, 34), :].astype(BF)
            out_ref[2 * w + x, :, 128:] = trials


def ordered(ref):
    flip = ones_at(iota((O, O), 1) == iota((O, O), 0) % W * Z + iota((O, O), 0) // W)
    tiles = [jnp.concatenate([ref[2 * w + x, :, 128:] for w in range(W)], 0) for x in range(2)]
    return [dot(flip, tile, 1, 0).astype(BF) for tile in tiles]


def place(ref, c, trials_ref):
    for x, tile in enumerate(ordered(ref)):
        for z in range(Z):
            start = pl.multiple_of(64 * z + 32 * x + BLK * c, BLK)
            trials_ref[pl.ds(start, BLK), :] = tile[W * z : W * (z + 1), :]


def own_kernel(at_ref, own_ref, virtual_hbm, trials_ref, virtual_ref, sems):
    copies = []
    for k in range(4):
        part = pl.ds(4 * k, 4)
        copies.append(pltpu.make_async_copy(virtual_hbm.at[part], virtual_ref.at[part], sems.at[k]))
        copies[k].start()
    place(own_ref, at_ref[0], trials_ref)
    for copy in copies:
        copy.wait()


def partial(of, screened_ref, trials_ref, virtual_ref, out_ref):
    rows = jnp.concatenate([virtual_ref[:, 2 * x + of].reshape(O, V) for x in range(2)], 0)
    halves = dot(rows, trials_ref[...], 1, 0).astype(BF)
    for x in range(2):
        part = dot(screened_ref[...], halves[O * x : O * (x + 1), :], 1, 1).astype(out_ref.dtype)
        for w in range(W):
            out_ref[2 * w + x] = part[BLK * w : BLK * (w + 1), :]


def send_kernel(at_ref, own_ref, part_ref, other_ref, virtual_ref, send_ref, screened_ref, trials_ref):
    core = at_ref[0]
    here = iota((BLK, 128), 1) // 64 == core
    for w in range(W):
        for x in range(2):
            moved = pltpu.roll(other_ref[2 * w + x, :, :128].astype(F32), 64, 1)
            tile = jnp.where(here, own_ref[2 * w + x, :, :128].astype(F32), moved)
            screened_ref[BLK * w : BLK * (w + 1), 128 * x : 128 * (x + 1)] = tile.astype(BF)
    place(other_ref, 1 - core, trials_ref)
    partial(1 - core, screened_ref, trials_ref, virtual_ref, send_ref)


def keep_kernel(at_ref, screened_ref, trials_ref, virtual_ref, keep_ref):
    partial(at_ref[0], screened_ref, trials_ref, virtual_ref, keep_ref)


def add_kernel(kept_ref, got_ref, out_ref):
    out_ref[...] = (kept_ref[...] + got_ref[...].astype(F32)).astype(BF)


def fourth_kernel(got_ref, out_ref):
    total = jnp.sum(got_ref[...].astype(F32), 0)
    row, chunk = iota((8, 128), 0), iota((8, 128), 1) // BLK
    for r in range(2):
        for h in range(2):
            t = total[8 * r : 8 * (r + 1), 128 * h : 128 * (h + 1)]
            for s in (1, 2, 4):
                up = pltpu.roll(pltpu.roll(t, 8 - s, 0), BLK * s, 1)
                down = pltpu.roll(pltpu.roll(t, s, 0), 128 - BLK * s, 1)
                high, right = row & s != 0, chunk & s != 0
                t = jnp.where(high == right, t, jnp.where(right, up, down))
            out_ref[8 * h : 8 * (h + 1), r, :] = t


def last_kernel(got_ref, out_ref):
    rows = []
    for r in range(2):
        total = jnp.sum(got_ref[:, r, :], 0, keepdims=True)
        t = jnp.where(iota((8, 128), 0) == iota((8, 128), 1) // BLK, total, 0.0)
        for s in (64, 32, BLK):
            t = t + pltpu.roll(t, s, 1)
        rows.append(t)
    out_ref[...] = jnp.concatenate(rows, 0).T[:BLK, :].reshape(BLK, 1, BLK)


def in_vmem(v):
    return pltpu.with_memory_space_constraint(v, pltpu.VMEM)


def in_hbm(v):
    return pltpu.with_memory_space_constraint(v, pltpu.HBM)


def vmem_out(shape, dtype):
    return pltpu.VMEM(shape, dtype)


def call(body, outs, *args, scratch=(), limit=24 << 20, hbm=(), alias={}):
    vmem = pl.BlockSpec(memory_space=pltpu.VMEM)
    specs = [pl.BlockSpec(memory_space=pltpu.SMEM) if a.dtype == jnp.int32 else vmem for a in args]
    for at in hbm:
        specs[at] = pl.BlockSpec(memory_space=pltpu.HBM)
    return pl.pallas_call(
        body,
        out_shape=outs,
        in_specs=specs,
        out_specs=jax.tree.map(lambda o: vmem, outs),
        scratch_shapes=scratch,
        compiler_params=pltpu.CompilerParams(vmem_limit_bytes=limit),
        input_output_aliases=alias,
        name=body.__name__,
    )(*args)


def swap(v, axis):
    return in_vmem(lax.all_to_all(v, axis, 0, 0, tiled=True))


def across(v):
    return in_vmem(lax.ppermute(v, "c", [(0, 1), (1, 0)]))


def per_device(pair_integrals, screening, virtual_integrals, trials):
    at = lax.axis_index(("xh", "y")).reshape(1).astype(jnp.int32)
    core = lax.axis_index("c").reshape(1).astype(jnp.int32)
    sent = call(
        first_kernel,
        vmem_out((Z, 17, 2, 128), BF),
        at,
        in_hbm(pair_integrals),
        in_hbm(screening),
        in_hbm(trials.reshape(O, BLK).T),
        scratch=[
            pltpu.VMEM((64, V), BF),
            pltpu.VMEM((V, V), BF),
            pltpu.VMEM((BLK, O), BF),
            pltpu.VMEM((W * STEP, 64), F32),
            pltpu.SemaphoreType.DMA((10,)),
        ],
        hbm=(1, 2, 3),
    )
    got = swap(sent, "z")
    sent = call(second_kernel, vmem_out((2 * W, Z, 384), BF), got, scratch=[pltpu.VMEM((Z * 34, 128), F32)])
    own = swap(sent, XY)
    other = across(own)
    own_trials, virtual = call(
        own_kernel,
        (vmem_out((V, O), BF), vmem_out((Z, 4, BLK, V), BF)),
        core,
        own,
        in_hbm(virtual_integrals.reshape(Z, 4, BLK, V)),
        scratch=[pltpu.SemaphoreType.DMA((4,))],
        hbm=(2,),
    )
    sent, screened, whole = call(
        send_kernel,
        (vmem_out((2 * W, BLK, O), BF), vmem_out((O, O), BF), vmem_out((V, O), BF)),
        core,
        own,
        own_trials,
        other,
        virtual,
        alias={2: 2},
    )
    got = across(sent)
    kept = call(keep_kernel, vmem_out((2 * W, BLK, O), F32), core, screened, whole, virtual)
    got = swap(call(add_kernel, vmem_out((2 * W, BLK, O), BF), kept, got), XY)
    got = swap(call(fourth_kernel, vmem_out((Z, 2, 128), F32), got), "z")
    return call(last_kernel, jax.ShapeDtypeStruct((BLK, 1, BLK), F32), got)


def solution(mesh):
    chips = Mesh(mesh.devices.reshape(2, 8, 16, 2, 2), ALL)
    return jax.shard_map(
        per_device,
        mesh=chips,
        in_specs=(
            P(ALL, None),
            P(),
            P(ALL, None, None),
            P(None, None, ("z", "xl", "c")),
        ),
        out_specs=P(("z", "xl", "c"), None, ("xh", "y")),
        check_vma=False,
    )
```

```python
import jax
import jax.numpy as jnp
from jax import lax
from jax.experimental import pallas as pl
from jax.experimental.pallas import tpu as pltpu
from jax.sharding import Mesh, PartitionSpec as P

O = 256
V = 1024
W = 16
Z = 16
BLK = 16
STEP = 72
XY = ("xh", "y", "xl")
ALL = ("xh", "y", "z", "xl", "c")
BF = jnp.bfloat16
F32 = jnp.float32


def iota(shape, axis):
    return lax.broadcasted_iota(jnp.int32, shape, axis)


def ones_at(mask, dtype=BF):
    return jnp.where(mask, 1.0, 0.0).astype(dtype)


def dot(a, b, ca, cb, precision=None):
    return lax.dot_general(
        a, b, (((ca,), (cb,)), ((), ())), precision=precision, preferred_element_type=F32
    )


def first_kernel(
    at_ref, pairs_hbm, screening_hbm, trials_hbm, out_ref, pairs_ref, screening_ref, trials_ref, columns_ref, sems
):
    copies = [pltpu.make_async_copy(pairs_hbm, pairs_ref, sems.at[0])]
    for k in range(8):
        part = (pl.ds(O * (k % 4), O), pl.ds(O * 2 * (k // 4), O * 2))
        copies.append(pltpu.make_async_copy(screening_hbm.at[part], screening_ref.at[part], sems.at[1 + k]))
    copies.append(pltpu.make_async_copy(trials_hbm, trials_ref, sems.at[9]))
    for copy in copies:
        copy.start()
    copies[0].wait()
    for k in range(2):
        for r in range(4):
            copies[1 + 4 * k + r].wait()
        columns = dot(pairs_ref[...], screening_ref[:, O * 2 * k : O * 2 * (k + 1)], 1, 0).T
        for w in range(8):
            columns_ref[pl.ds(STEP * (8 * k + w), 64), :] = columns[64 * w : 64 * (w + 1), :]
    copies[9].wait()
    mine = iota((BLK, O), 0) == at_ref[0]
    row = jnp.sum(jnp.where(mine, trials_ref[...].astype(F32), 0.0), 0, keepdims=True)
    tail = jnp.where(iota((2, 128), 0) == 0, row[:, :128], row[:, 128:]).astype(BF)
    for z in range(Z):
        for x in range(2):
            left, right = (columns_ref[pl.ds(4 * z + 2 * x + c, W, STEP), :] for c in range(2))
            out_ref[z, 8 * x : 8 * (x + 1)] = jnp.concatenate([left, right], 1).astype(BF).reshape(8, 2, 128)
        out_ref[z, 16] = tail


def second_kernel(got_ref, out_ref, rows_ref):
    rows_ref[...] = got_ref[...].reshape(Z * 34, 128).astype(F32)
    trials = jnp.concatenate([rows_ref[pl.ds(r, Z, 34), :] for r in (32, 33)], 1).astype(BF)
    for w in range(W):
        for x in range(2):
            out_ref[2 * w + x, :, :128] = rows_ref[pl.ds(W * x + w, Z, 34), :].astype(BF)
            out_ref[2 * w + x, :, 128:] = trials


def ordered(ref):
    flip = ones_at(iota((O, O), 1) == iota((O, O), 0) % W * Z + iota((O, O), 0) // W)
    tiles = [jnp.concatenate([ref[2 * w + x, :, 128:] for w in range(W)], 0) for x in range(2)]
    return [dot(flip, tile, 1, 0).astype(BF) for tile in tiles]


def place(ref, c, trials_ref):
    for x, tile in enumerate(ordered(ref)):
        for z in range(Z):
            start = pl.multiple_of(64 * z + 32 * x + BLK * c, BLK)
            trials_ref[pl.ds(start, BLK), :] = tile[W * z : W * (z + 1), :]


def own_kernel(at_ref, own_ref, trials_ref):
    place(own_ref, at_ref[0], trials_ref)


def partial(of, screened_ref, trials_ref, virtual_ref, out_ref):
    rows = jnp.concatenate([virtual_ref[:, 2 * x + of].reshape(O, V) for x in range(2)], 0)
    halves = dot(rows, trials_ref[...], 1, 0).astype(BF)
    for x in range(2):
        part = dot(screened_ref[...], halves[O * x : O * (x + 1), :], 1, 1).astype(out_ref.dtype)
        for w in range(W):
            out_ref[2 * w + x] = part[BLK * w : BLK * (w + 1), :]


def send_kernel(at_ref, own_ref, part_ref, other_ref, virtual_ref, send_ref, screened_ref, trials_ref):
    core = at_ref[0]
    here = iota((BLK, 128), 1) // 64 == core
    for w in range(W):
        for x in range(2):
            moved = pltpu.roll(other_ref[2 * w + x, :, :128].astype(F32), 64, 1)
            tile = jnp.where(here, own_ref[2 * w + x, :, :128].astype(F32), moved)
            screened_ref[BLK * w : BLK * (w + 1), 128 * x : 128 * (x + 1)] = tile.astype(BF)
    place(other_ref, 1 - core, trials_ref)
    partial(1 - core, screened_ref, trials_ref, virtual_ref, send_ref)


def keep_kernel(at_ref, screened_ref, trials_ref, virtual_ref, keep_ref):
    partial(at_ref[0], screened_ref, trials_ref, virtual_ref, keep_ref)


def add_kernel(kept_ref, got_ref, out_ref):
    out_ref[...] = (kept_ref[...] + got_ref[...].astype(F32)).astype(BF)


def fourth_kernel(got_ref, out_ref):
    total = jnp.sum(got_ref[...].astype(F32), 0)
    row, chunk = iota((8, 128), 0), iota((8, 128), 1) // BLK
    for r in range(2):
        for h in range(2):
            t = total[8 * r : 8 * (r + 1), 128 * h : 128 * (h + 1)]
            for s in (1, 2, 4):
                up = pltpu.roll(pltpu.roll(t, 8 - s, 0), BLK * s, 1)
                down = pltpu.roll(pltpu.roll(t, s, 0), 128 - BLK * s, 1)
                high, right = row & s != 0, chunk & s != 0
                t = jnp.where(high == right, t, jnp.where(right, up, down))
            out_ref[8 * h : 8 * (h + 1), r, :] = t


def last_kernel(got_ref, out_ref):
    rows = []
    for r in range(2):
        total = jnp.sum(got_ref[:, r, :], 0, keepdims=True)
        t = jnp.where(iota((8, 128), 0) == iota((8, 128), 1) // BLK, total, 0.0)
        for s in (64, 32, BLK):
            t = t + pltpu.roll(t, s, 1)
        rows.append(t)
    out_ref[...] = jnp.concatenate(rows, 0).T[:BLK, :].reshape(BLK, 1, BLK)


def in_vmem(v):
    return pltpu.with_memory_space_constraint(v, pltpu.VMEM)


def in_hbm(v):
    return pltpu.with_memory_space_constraint(v, pltpu.HBM)


def vmem_out(shape, dtype):
    return pltpu.VMEM(shape, dtype)


def call(body, outs, *args, scratch=(), limit=24 << 20, hbm=(), alias={}):
    vmem = pl.BlockSpec(memory_space=pltpu.VMEM)
    specs = [pl.BlockSpec(memory_space=pltpu.SMEM) if a.dtype == jnp.int32 else vmem for a in args]
    for at in hbm:
        specs[at] = pl.BlockSpec(memory_space=pltpu.HBM)
    return pl.pallas_call(
        body,
        out_shape=outs,
        in_specs=specs,
        out_specs=jax.tree.map(lambda o: vmem, outs),
        scratch_shapes=scratch,
        compiler_params=pltpu.CompilerParams(vmem_limit_bytes=limit),
        input_output_aliases=alias,
        name=body.__name__,
    )(*args)


def swap(v, axis):
    return in_vmem(lax.all_to_all(v, axis, 0, 0, tiled=True))


def across(v):
    return in_vmem(lax.ppermute(v, "c", [(0, 1), (1, 0)]))


def per_device(pair_integrals, screening, virtual_integrals, trials):
    at = lax.axis_index(("xh", "y")).reshape(1).astype(jnp.int32)
    core = lax.axis_index("c").reshape(1).astype(jnp.int32)
    sent = call(
        first_kernel,
        vmem_out((Z, 17, 2, 128), BF),
        at,
        in_hbm(pair_integrals),
        in_hbm(screening),
        in_hbm(trials.reshape(O, BLK).T),
        scratch=[
            pltpu.VMEM((64, V), BF),
            pltpu.VMEM((V, V), BF),
            pltpu.VMEM((BLK, O), BF),
            pltpu.VMEM((W * STEP, 64), F32),
            pltpu.SemaphoreType.DMA((10,)),
        ],
        hbm=(1, 2, 3),
    )
    got = swap(sent, "z")
    sent = call(second_kernel, vmem_out((2 * W, Z, 384), BF), got, scratch=[pltpu.VMEM((Z * 34, 128), F32)])
    own = swap(sent, XY)
    other = across(own)
    own_trials = call(own_kernel, vmem_out((V, O), BF), core, own)
    virtual = in_vmem(virtual_integrals.reshape(Z, 4, BLK, V))
    sent, screened, whole = call(
        send_kernel,
        (vmem_out((2 * W, BLK, O), BF), vmem_out((O, O), BF), vmem_out((V, O), BF)),
        core,
        own,
        own_trials,
        other,
        virtual,
        alias={2: 2},
    )
    got = across(sent)
    kept = call(keep_kernel, vmem_out((2 * W, BLK, O), F32), core, screened, whole, virtual)
    got = swap(call(add_kernel, vmem_out((2 * W, BLK, O), BF), kept, got), XY)
    got = swap(call(fourth_kernel, vmem_out((Z, 2, 128), F32), got), "z")
    return call(last_kernel, jax.ShapeDtypeStruct((BLK, 1, BLK), F32), got)


def solution(mesh):
    chips = Mesh(mesh.devices.reshape(2, 8, 16, 2, 2), ALL)
    return jax.shard_map(
        per_device,
        mesh=chips,
        in_specs=(
            P(ALL, None),
            P(),
            P(ALL, None, None),
            P(None, None, ("z", "xl", "c")),
        ),
        out_specs=P(("z", "xl", "c"), None, ("xh", "y")),
        check_vma=False,
    )
```
